32 devices in a mesh: rep: 2 (over y), wide: 2 (over core), narrow: 8 (over z, x).
Axes of the slice: x: 2, y: 2, z: 4, core: 2. Of those that a mesh axis runs over, the one named last changes fastest.
Arguments:
- queries: bfloat16 [8, 120, 4096], P(('rep', 'wide'), None, 'narrow'), parts along dimension 0, may hold values from -6 to 6
- layer_rows: bfloat16 [8, 120, 4096], P(('rep', 'wide'), None, 'narrow'), parts along dimension 0, may hold values from -6 to 6
- positions: int32 [8, 120], P(('rep', 'wide')), parts along dimension 0, may hold values from 0 to 2047, as said below
- counts: int32 [8], P('rep'), parts along dimension 0, may hold values from 1 to 120, 300 in all
- key_cache: bfloat16 [8, 65536, 128], P(('rep', 'wide'), 'narrow'), parts along dimension 0, may hold values from -400 to 400
- value_cache: bfloat16 [8, 65536, 128], P(('rep', 'wide'), 'narrow'), parts along dimension 0, may hold values from -6 to 6
- out_weight: bfloat16 [4096, 4096], P(None, 'narrow'), may hold values from -0.09375 to 0.09375
- ffn_gain: bfloat16 [4096], replicated, may hold values from 0.5 to 2
- w_gate: bfloat16 [12288, 4096], P('narrow'), may hold values from -0.09375 to 0.09375
- w_up: bfloat16 [12288, 4096], P('narrow'), may hold values from -0.09375 to 0.09375
- w_down: bfloat16 [4096, 12288], P('narrow'), may hold values from -0.0546875 to 0.0546875
Outputs:
- refreshed: bfloat16 [600, 4096], P(('rep', 'wide'), 'narrow'), parts along dimension 0
The draws below stay inside these ranges and needn't reach their ends.
There are 2 independent parts, one for each index of `rep`. The reference program is written for one: setup_inputs(seed, part) draws one part's arguments, and reference() takes and returns one part's arrays. A program takes and returns all parts, laid end to end along the dimension named above; an argument that names none is the same for every part. Nothing has to cross between parts.
Inputs may be any that keep to these rules, and one draw needn't show every extreme that they name: Within each canvas the 120 slot positions are distinct. The live slots of a canvas are its first counts slots. The counts are taken part by part: the 4 counts of each part sum to 150 times the number of wide groups, so an array that holds several parts sums to that once for each part.
All inputs are finite; a program needn't handle non-finite values.
Results may differ from the reference program's by a relative error of at most 0.012.
The reference program's roundings to bfloat16 on the way (of `rotated`, `weights`, `attended`, `residual`, `balanced`, `normed` and `activated`) count: a program that leaves them out, or rounds other values in their place, can miss the bound.
Values may be sent and summed in bfloat16 or wider, within the bound.
No kernel may reach another device: no remote copies, remote signals or barrier semaphores. Data moves between devices by JAX's collectives and lax.ppermute only.
A program may use at most 128 MiB of HBM per device.

```python
import math
import jax
import jax.numpy as jnp
import numpy as np
from jax import lax

D = 4096
FF = 12288
HEAD = 128
LEN = 2048
RCAP = 120
NC = 4
BAL = 150
N_WIDE = 2


def draw_positions(key, part):
    canvas_keys = jax.random.split(key, NC)

    def one_canvas(canvas_key):
        order_key, spot_key = jax.random.split(canvas_key)
        shuffled = jax.random.permutation(order_key, LEN)[:RCAP]
        lifted = jax.random.randint(spot_key, (), 0, RCAP)
        offset = LEN - 1 - shuffled[lifted]
        return ((shuffled + offset) % LEN).astype(jnp.int32)
    return jax.vmap(one_canvas)(canvas_keys)


def draw_key_cache(key, part):
    head_count = D // HEAD
    values = jnp.clip(jax.random.normal(key, (NC, head_count * LEN, HEAD), jnp.float32), -6.0, 6.0) * 2.5
    return values.astype(jnp.bfloat16)


def shard_levels(rng, shape, cuts, low, high):
    loudness, own = 1.0, jax.random.fold_in(rng, 6)
    for axis_at, blocks in cuts:
        heights = jnp.exp(jax.random.uniform(jax.random.fold_in(own, axis_at), (blocks,), jnp.float32, low / len(cuts), high / len(cuts)))
        loudness = loudness * jnp.repeat(heights, shape[axis_at] // blocks).reshape([-1 if axis == axis_at else 1 for axis in range(len(shape))])
    return loudness


def split_up(amount, total, most, slope):
    weights = [(1 << 20) // math.isqrt(standing ** slope) + 1 for standing in range(2, amount + 1)]
    surplus, holding = total - most - (amount - 1), [1] * (amount - 1)
    while surplus > 0:
        free = [i for i in range(amount - 1) if holding[i] < most]
        mass, remaining = sum([weights[i] for i in free]), surplus
        for i in free:
            more = min(most - holding[i], max(1, remaining * weights[i] // mass), surplus)
            holding[i] = holding[i] + more
            surplus = surplus - more
    return np.array([most] + holding)


def ragged_sizes(stream_key, number_of, total, most, lean):
    if number_of == 2:
        one = jax.random.randint(stream_key, (), max(1, total - most), min(most, total - 1) + 1)
        return jnp.stack([one, total - one])
    tallies = jnp.asarray(split_up(number_of, total, most, lean), jnp.int32)
    pairs = (number_of - 1) // 2
    donor, taker = tallies[1:1 + 2 * pairs:2], tallies[2:2 + 2 * pairs:2]
    slack = jnp.minimum(donor - 1, most - taker)
    shifted = jax.random.randint(jax.random.fold_in(stream_key, 1), (pairs,), 0, 1 << 20) % (slack + 1)
    tallies = tallies.at[1:1 + 2 * pairs:2].set(donor - shifted).at[2:2 + 2 * pairs:2].set(taker + shifted)
    return tallies[jax.random.permutation(jax.random.fold_in(stream_key, 2), number_of)]


def noise(own_key, extent, deviation, bound, cuts=(), kind=jnp.bfloat16):
    gain = shard_levels(own_key, extent, cuts, -0.22, 0.18) if cuts else 1.0
    result = jax.random.normal(own_key, extent, jnp.float32) * deviation * gain
    return jnp.minimum(jnp.maximum(result, -bound), bound).astype(kind)


def setup_inputs(seed: int = 0, part: int = 0) -> dict:
    key_of = jax.random.split(jax.random.key(seed), 12)
    part_splits = jax.random.split(jax.random.fold_in(key_of[11], part), 12)
    queries = noise(part_splits[0], (NC, RCAP, D), 1.0, 6.0, ((0, 2), (2, 8)))
    layer_rows = noise(part_splits[1], (NC, RCAP, D), 1.0, 6.0, ((0, 2), (2, 8)))
    positions = draw_positions(jax.random.fold_in(jax.random.fold_in(key_of[11], part), 71), part)
    counts = ragged_sizes(part_splits[3], NC, N_WIDE * BAL, RCAP, 2).astype(jnp.int32)
    key_cache = draw_key_cache(jax.random.fold_in(jax.random.fold_in(key_of[11], part), 71), part)
    value_cache = noise(part_splits[5], (NC, (D // HEAD) * LEN, HEAD), 1.0, 6.0, ((0, 2), (1, 8)))
    out_weight = noise(key_of[6], (D, D), D ** -0.5, 0.09375, ((1, 8),))
    ffn_gain = jnp.clip(jnp.exp(jax.random.uniform(key_of[7], (D,), jnp.float32, math.log(0.5), math.log(2.0))), 0.5, 2.0).astype(jnp.bfloat16)
    w_gate = noise(key_of[8], (FF, D), D ** -0.5, 0.09375, ((0, 8),))
    w_up = noise(key_of[9], (FF, D), D ** -0.5, 0.09375, ((0, 8),))
    w_down = noise(key_of[10], (D, FF), FF ** -0.5, 0.0546875, ((0, 8),))
    return {"queries": queries, "layer_rows": layer_rows, "positions": positions, "counts": counts, "key_cache": key_cache, "value_cache": value_cache, "out_weight": out_weight, "ffn_gain": ffn_gain, "w_gate": w_gate, "w_up": w_up, "w_down": w_down}


epsilon = 1e-05

def rotate_queries(queries_f32, positions):
    half_size = HEAD // 2
    frequency = 500000.0 ** (-2.0 * jnp.arange(half_size, dtype=jnp.float32) / HEAD)
    angles = positions.astype(jnp.float32)[..., None] * frequency
    cosine_table = jnp.cos(angles)[..., None, :]
    sine_table = jnp.sin(angles)[..., None, :]
    lower_half = queries_f32[..., :half_size]
    upper_half = queries_f32[..., half_size:]
    return jnp.concatenate([lower_half * cosine_table - upper_half * sine_table, upper_half * cosine_table + lower_half * sine_table], axis=-1)

def attend_canvas(inputs):
    query_rows, key_rows, value_rows = inputs
    head_count = D // HEAD
    key_heads = key_rows.astype(jnp.float32).reshape(head_count, LEN, HEAD)
    value_heads = value_rows.astype(jnp.float32).reshape(head_count, LEN, HEAD)
    query_heads = query_rows.astype(jnp.float32).reshape(RCAP, head_count, HEAD)
    scores = jnp.einsum('rhd,hpd->hrp', query_heads, key_heads) * HEAD ** (-0.5)
    row_peak = lax.optimization_barrier(jnp.max(scores, axis=2, keepdims=True))
    exponent = jnp.exp(scores - row_peak)
    totals = lax.optimization_barrier(jnp.sum(exponent, axis=2))
    weights = exponent.astype(jnp.bfloat16)
    mixture = jnp.einsum('hrp,hpd->rhd', weights.astype(jnp.float32), value_heads)
    attended = mixture / jnp.transpose(totals)[:, :, None]
    return attended.reshape(RCAP, D).astype(jnp.bfloat16)

def reference(queries, layer_rows, positions, counts, key_cache, value_cache, out_weight, ffn_gain, w_gate, w_up, w_down):
    head_count = D // HEAD
    canvas_count = queries.shape[0]
    rotated = rotate_queries(queries.astype(jnp.float32).reshape(canvas_count, RCAP, head_count, HEAD), positions)
    rotated = rotated.reshape(canvas_count, RCAP, D).astype(jnp.bfloat16)
    attended = lax.map(attend_canvas, (rotated, key_cache, value_cache))
    projected = jnp.dot(attended.reshape(-1, D), out_weight, preferred_element_type=jnp.float32)
    residual = (layer_rows.reshape(-1, D).astype(jnp.float32) + projected).astype(jnp.bfloat16)
    canvas_end = jnp.cumsum(counts, dtype=jnp.int32)
    canvas_start = canvas_end - counts
    global_slot = jnp.arange(N_WIDE * BAL, dtype=jnp.int32)
    canvas_of = lax.optimization_barrier(jnp.sum((canvas_end[None, :] <= global_slot[:, None]).astype(jnp.int32), axis=1, dtype=jnp.int32))
    within = global_slot - canvas_start[canvas_of]
    flat_slot = (canvas_of * RCAP + within).astype(jnp.int32)
    balanced = residual[flat_slot]
    balanced_f32 = balanced.astype(jnp.float32)
    normed = (balanced_f32 * lax.rsqrt(lax.optimization_barrier(jnp.mean(balanced_f32 * balanced_f32, axis=1, keepdims=True)) + epsilon) * ffn_gain.astype(jnp.float32)).astype(jnp.bfloat16)
    gate_sum = jnp.dot(normed, w_gate.T, preferred_element_type=jnp.float32)
    up_sum = jnp.dot(normed, w_up.T, preferred_element_type=jnp.float32)
    activated = (jax.nn.silu(gate_sum) * up_sum).astype(jnp.bfloat16)
    refreshed = (balanced_f32 + jnp.dot(activated, w_down.T, preferred_element_type=jnp.float32)).astype(jnp.bfloat16)
    return refreshed
```

```python
import functools

import jax
import jax.numpy as jnp
from jax import lax
from jax.experimental import pallas as pl
from jax.experimental.pallas import tpu as pltpu
from jax.sharding import PartitionSpec as P

D = 4096
HEAD = 128
BAL = 150
CHUNKS = 3

epsilon = 1e-05
BF = jnp.bfloat16
F32 = jnp.float32


def from_partner(x, axis, distance):
    return lax.ppermute(x, axis, [(i, i ^ 1 << distance) for i in range(lax.axis_size(axis))])


def rotate_queries(queries_f32, positions):
    half_size = HEAD // 2
    frequency = 500000.0 ** (-2.0 * jnp.arange(half_size, dtype=jnp.float32) / HEAD)
    angles = positions.astype(jnp.float32)[..., None] * frequency
    cosine_table = jnp.cos(angles)[..., None, :]
    sine_table = jnp.sin(angles)[..., None, :]
    lower_half = queries_f32[..., :half_size]
    upper_half = queries_f32[..., half_size:]
    return jnp.concatenate(
        [
            lower_half * cosine_table - upper_half * sine_table,
            upper_half * cosine_table + lower_half * sine_table,
        ],
        axis=-1,
    )


def balanced_slots(counts, canvases, slot_cap, groups, share):
    canvas_total = counts.shape[0]
    canvas_end = jnp.cumsum(counts, dtype=jnp.int32)
    canvas_start = canvas_end - counts
    global_slot = jnp.arange(groups * share, dtype=jnp.int32)
    canvas_of = jnp.sum(
        (canvas_end[None, :] <= global_slot[:, None]).astype(jnp.int32), axis=1, dtype=jnp.int32
    )
    canvas_of = jnp.minimum(canvas_of, canvas_total - 1)
    matches = canvas_of[:, None] == jnp.arange(canvas_total, dtype=jnp.int32)[None, :]
    picked_start = jnp.sum(jnp.where(matches, canvas_start[None, :], 0), axis=1, dtype=jnp.int32)
    within = global_slot - picked_start
    source = canvas_of // canvases
    local_slot = canvas_of % canvases * slot_cap + within
    return (source.reshape(groups, share), local_slot.reshape(groups, share))


def route_rows(rows_local, counts, canvases, slot_cap, groups, share):
    source, local_slot = balanced_slots(counts, canvases, slot_cap, groups, share)
    from_here = source == lax.axis_index("wide")
    picked = jnp.take(rows_local, jnp.where(from_here, local_slot, 0).reshape(-1), axis=0)
    picked = picked.reshape(groups, share, rows_local.shape[1])
    return jnp.where(from_here[:, :, None], picked, jnp.zeros_like(picked))


def feed_forward(residual, ffn_gain, w_gate, w_up, w_down):
    gathered = lax.all_gather(residual, "narrow", axis=1, tiled=True).astype(jnp.float32)
    normed = (
        gathered
        * lax.rsqrt(jnp.mean(gathered * gathered, axis=1, keepdims=True) + epsilon)
        * ffn_gain.astype(jnp.float32)
    ).astype(jnp.bfloat16)
    contract = (((1,), (1,)), ((), ()))
    gate_sum = lax.dot_general(normed, w_gate, contract, preferred_element_type=jnp.float32)
    up_sum = lax.dot_general(normed, w_up, contract, preferred_element_type=jnp.float32)
    activated = (jax.nn.silu(gate_sum) * up_sum).astype(jnp.bfloat16)
    output = lax.dot_general(
        lax.all_gather(activated, "narrow", axis=1, tiled=True),
        w_down,
        contract,
        preferred_element_type=jnp.float32,
    )
    return (residual.astype(jnp.float32) + output).astype(jnp.bfloat16)


def general_device(
    queries,
    layer_rows,
    positions,
    counts,
    key_cache,
    value_cache,
    out_weight,
    ffn_gain,
    w_gate,
    w_up,
    w_down,
):
    canvases, slot_cap, feature_share = queries.shape
    head_count = D // HEAD
    narrow_count = lax.axis_size("narrow")
    groups = lax.axis_size("wide")
    row_count = canvases * slot_cap
    group_size = max(1, narrow_count // head_count)
    local_heads = max(1, head_count // narrow_count)
    bit_steps = group_size.bit_length() - 1
    device_index = lax.axis_index("narrow")
    joined = queries
    for level in range(bit_steps):
        partner = from_partner(joined, "narrow", level)
        upper_bit = device_index // 2**level % 2 == 1
        joined = jnp.where(
            upper_bit,
            jnp.concatenate([partner, joined], axis=2),
            jnp.concatenate([joined, partner], axis=2),
        )
    rotated = rotate_queries(
        joined.astype(jnp.float32).reshape(canvases, slot_cap, local_heads, HEAD), positions
    ).astype(jnp.bfloat16)
    block_rows = key_cache.shape[1] // local_heads
    key_blocks = key_cache.reshape(canvases, local_heads, block_rows, HEAD)
    value_blocks = value_cache.reshape(canvases, local_heads, block_rows, HEAD)
    scores = jnp.einsum(
        "crhd,chpd->chrp", rotated, key_blocks, preferred_element_type=jnp.float32
    ) * HEAD ** (-0.5)
    row_peak = jnp.max(scores, axis=3)
    for level in range(bit_steps):
        other_peak = from_partner(row_peak, "narrow", level)
        row_peak = jnp.maximum(row_peak, other_peak)
    exponent = jnp.exp(scores - row_peak[..., None])
    totals = jnp.sum(exponent, axis=3)
    mixture = jnp.einsum(
        "chrp,chpd->crhd",
        exponent.astype(jnp.bfloat16),
        value_blocks,
        preferred_element_type=jnp.float32,
    ).reshape(row_count, local_heads * HEAD)
    for level in reversed(range(bit_steps)):
        half_width = mixture.shape[1] // 2
        lower_part = mixture[:, :half_width]
        upper_part = mixture[:, half_width:]
        upper_bit = device_index // 2**level % 2 == 1
        outgoing = jnp.where(upper_bit, lower_part, upper_part)
        kept = jnp.where(upper_bit, upper_part, lower_part)
        arrived, arrived_totals = from_partner((outgoing, totals), "narrow", level)
        mixture = kept + arrived
        totals = totals + arrived_totals
    divisor = jnp.repeat(
        jnp.transpose(totals, (0, 2, 1)).reshape(row_count, local_heads),
        mixture.shape[1] // local_heads,
        axis=1,
    )
    attended = (mixture / divisor).astype(jnp.bfloat16)
    projected = jnp.dot(
        lax.all_gather(attended, "narrow", axis=1, tiled=True),
        out_weight,
        preferred_element_type=jnp.float32,
    )
    residual = (
        layer_rows.reshape(row_count, feature_share).astype(jnp.float32) + projected
    ).astype(jnp.bfloat16)
    outgoing_rows = route_rows(residual, counts, canvases, slot_cap, groups, BAL)
    incoming = lax.all_to_all(outgoing_rows, "wide", split_axis=0, concat_axis=0, tiled=True)
    balanced = jnp.sum(incoming.astype(jnp.float32), axis=0).astype(jnp.bfloat16)
    return feed_forward(balanced, ffn_gain, w_gate, w_up, w_down)


def attend_kernel(
    slots, spill, counts, place, q_ref, cos_ref, sin_ref, k_ref, v_ref, rows_ref, own_ref, out_ref
):
    canvas = pl.program_id(1)
    canvases = pl.num_programs(1)
    wide = place[0]
    q = q_ref[0].astype(F32)
    half = HEAD // 2
    rotated = (q * cos_ref[0] + pltpu.roll(q, half, 1) * sin_ref[0]).astype(BF)
    scores = lax.dot_general(
        rotated, k_ref[0], (((1,), (1,)), ((), ())), preferred_element_type=F32
    ) * HEAD ** (-0.5)
    peak = jnp.max(scores, axis=1, keepdims=True)
    exponent = jnp.exp(scores - peak)
    total = jnp.sum(exponent, axis=1, keepdims=True)
    mixture = jnp.dot(exponent.astype(BF), v_ref[0], preferred_element_type=F32)
    attended = (mixture / total).astype(BF)

    mine = wide * canvases + canvas
    start = jnp.int32(0)
    for c in range(counts.shape[0]):
        start += jnp.where(c < mine, counts[c], 0)
    live = counts[mine]
    slot_cap = q.shape[0]

    def pick(size, shift):
        at = lax.broadcasted_iota(jnp.int32, (size, slot_cap), 0)
        slot = lax.broadcasted_iota(jnp.int32, (size, slot_cap), 1)
        return jnp.where((at == slot + shift) & (slot < live), 1.0, 0.0).astype(BF)

    pick_own = pick(slots, start - wide * slots)
    pick_out = pick(spill, start - (1 - wide) * slots - wide * (slots - spill))
    for i, value in enumerate((attended, rows_ref[0])):
        own = jnp.dot(pick_own, value, preferred_element_type=F32).astype(BF)
        out = jnp.dot(pick_out, value, preferred_element_type=F32).astype(BF)

        @pl.when(canvas == 0)
        def _():
            own_ref[i] = own
            out_ref[i] = out

        @pl.when(canvas > 0)
        def _():
            own_ref[i] += own
            out_ref[i] += out


def attend(queries, layer_rows, positions, counts, key_cache, value_cache, spill):
    canvases, slot_cap, features = queries.shape
    heads = features // HEAD
    length = key_cache.shape[1] // heads
    half = HEAD // 2
    frequency = 500000.0 ** (-2.0 * jnp.arange(half, dtype=F32) / HEAD)
    angles = positions.astype(F32)[..., None] * frequency
    cosine = jnp.cos(angles)
    sine = jnp.sin(angles)
    cosine = jnp.concatenate([cosine, cosine], axis=-1)
    sine = jnp.concatenate([-sine, sine], axis=-1)
    place = lax.axis_index("wide").astype(jnp.int32).reshape(1)
    table = pl.BlockSpec((1, slot_cap, HEAD), lambda h, c, *_: (c, 0, 0))
    rows = pl.BlockSpec((1, slot_cap, HEAD), lambda h, c, *_: (c, 0, h))
    cache = pl.BlockSpec((1, length, HEAD), lambda h, c, *_: (c, h, 0))
    return pl.pallas_call(
        functools.partial(attend_kernel, BAL, spill),
        grid_spec=pltpu.PrefetchScalarGridSpec(
            num_scalar_prefetch=2,
            grid=(heads, canvases),
            in_specs=[rows, table, table, cache, cache, rows],
            out_specs=[
                pl.BlockSpec((2, BAL, HEAD), lambda h, c, *_: (0, 0, h)),
                pl.BlockSpec((2, spill, HEAD), lambda h, c, *_: (0, 0, h)),
            ],
        ),
        out_shape=[
            jax.ShapeDtypeStruct((2, BAL, features), BF),
            jax.ShapeDtypeStruct((2, spill, features), BF),
        ],
        compiler_params=pltpu.CompilerParams(vmem_limit_bytes=24 << 20),
        cost_estimate=pl.CostEstimate(
            flops=4 * canvases * slot_cap * features * length,
            bytes_accessed=4 * canvases * heads * length * HEAD,
            transcendentals=canvases * slot_cap * heads * length,
        ),
        name="attend",
    )(counts, place, queries, cosine, sine, key_cache, value_cache, layer_rows)


def project_kernel(n, block_of, contract, first, last, index, *refs):
    refs = list(refs)
    pieces = [refs.pop(0) for _ in range(n)]
    w_ref = refs.pop(0)
    acc_ref = None if first else refs.pop(0)
    base_ref = refs.pop(0) if last else None
    o_ref, held, sem = refs
    copies = []
    for i in range(n):
        copies.append(pltpu.make_async_copy(block_of(w_ref, index[i]), held.at[i], sem.at[i]))
        copies[-1].start()
    acc = None if first else acc_ref[...]
    for i in range(n):
        copies[i].wait()
        part = lax.dot_general(pieces[i][...], held[i], contract, preferred_element_type=F32)
        acc = part if acc is None else acc + part
    if last:
        acc = (base_ref[...].astype(F32) + acc).astype(BF)
    o_ref[...] = acc


def project(pieces, index, weight, block_of, block_shape, contract, columns, acc=None, base=None, name=None):
    n = len(pieces)
    rows = pieces[0].shape[0]
    vm = pl.BlockSpec(memory_space=pltpu.VMEM)
    operands = list(pieces) + [weight]
    specs = [vm] * n + [pl.BlockSpec(memory_space=pl.ANY)]
    for extra in (acc, base):
        if extra is not None:
            operands.append(extra)
            specs.append(vm)
    depth = pieces[0].shape[1]
    return pl.pallas_call(
        functools.partial(project_kernel, n, block_of, contract, acc is None, base is not None),
        in_specs=[pl.BlockSpec(memory_space=pltpu.SMEM)] + specs,
        out_specs=vm,
        out_shape=jax.ShapeDtypeStruct((rows, columns), F32 if base is None else BF),
        scratch_shapes=[
            pltpu.VMEM((n,) + block_shape, BF),
            pltpu.SemaphoreType.DMA((n,)),
        ],
        compiler_params=pltpu.CompilerParams(vmem_limit_bytes=24 << 20),
        cost_estimate=pl.CostEstimate(
            flops=2 * n * rows * depth * columns,
            bytes_accessed=2 * n * depth * columns,
            transcendentals=0,
        ),
        name=name,
    )(index, *operands)


def norm_kernel(n, index, *refs):
    pieces = refs[:n]
    gain_ref, o_ref = refs[n:]
    width = pieces[0].shape[1]
    total = 0.0
    for piece in pieces:
        value = piece[...].astype(F32)
        total = total + jnp.sum(value * value, axis=1, keepdims=True)
    scale = lax.rsqrt(total / (n * width) + epsilon)
    for i, piece in enumerate(pieces):
        at = pl.ds(pl.multiple_of(index[i] * width, width), width)
        value = piece[...].astype(F32) * scale * gain_ref[:, at].astype(F32)
        o_ref[:, at] = value.astype(BF)


def norm(pieces, index, gain):
    n = len(pieces)
    rows, width = pieces[0].shape
    vm = pl.BlockSpec(memory_space=pltpu.VMEM)
    return pl.pallas_call(
        functools.partial(norm_kernel, n),
        in_specs=[pl.BlockSpec(memory_space=pltpu.SMEM)] + [vm] * (n + 1),
        out_specs=vm,
        out_shape=jax.ShapeDtypeStruct((rows, n * width), BF),
        compiler_params=pltpu.CompilerParams(vmem_limit_bytes=24 << 20),
        cost_estimate=pl.CostEstimate(
            flops=6 * n * rows * width, bytes_accessed=4 * n * rows * width, transcendentals=rows
        ),
        name="norm",
    )(index, *pieces, gain.reshape(1, -1))


def hidden_kernel(x_ref, g_ref, u_ref, o_ref):
    contract = (((1,), (1,)), ((), ()))
    x = x_ref[...]
    gate = lax.dot_general(x, g_ref[...], contract, preferred_element_type=F32)
    up = lax.dot_general(x, u_ref[...], contract, preferred_element_type=F32)
    o_ref[...] = (gate / (1.0 + jnp.exp(-gate)) * up).astype(BF)


def hidden(normed, w_gate, w_up, begin, size, block):
    rows, depth = normed.shape
    weight = pl.BlockSpec((block, depth), lambda j: (begin // block + j, 0))
    return pl.pallas_call(
        hidden_kernel,
        grid=(size // block,),
        in_specs=[pl.BlockSpec((rows, depth), lambda j: (0, 0)), weight, weight],
        out_specs=pl.BlockSpec((rows, block), lambda j: (0, j)),
        out_shape=jax.ShapeDtypeStruct((rows, size), BF),
        compiler_params=pltpu.CompilerParams(vmem_limit_bytes=24 << 20),
        cost_estimate=pl.CostEstimate(
            flops=4 * rows * depth * size, bytes_accessed=4 * depth * size, transcendentals=rows * size
        ),
        name="hidden",
    )(normed, w_gate, w_up)


def spread(x):
    n = lax.axis_size("narrow")
    pieces = {0: x}
    for k in range(2, n, 2):
        pieces[k] = lax.ppermute(x, "narrow", [(i, i ^ k) for i in range(n)])
    swap = [(i, i ^ 1) for i in range(n)]
    for k in range(0, n, 2):
        pieces[k ^ 1] = lax.ppermute(pieces[k], "narrow", swap)
    return pieces


def local_device(
    queries,
    layer_rows,
    positions,
    counts,
    key_cache,
    value_cache,
    out_weight,
    ffn_gain,
    w_gate,
    w_up,
    w_down,
):
    canvases, slot_cap, share = queries.shape
    n = lax.axis_size("narrow")
    me = lax.axis_index("narrow").astype(jnp.int32)
    wide = lax.axis_index("wide")
    spill = canvases * slot_cap - BAL
    own, out = attend(queries, layer_rows, positions, counts, key_cache, value_cache, spill)
    arrived = lax.ppermute(out, "wide", [(0, 1), (1, 0)])
    gap = BAL - spill
    arrived = jnp.where(
        wide == 0,
        jnp.pad(arrived, ((0, 0), (gap, 0), (0, 0))),
        jnp.pad(arrived, ((0, 0), (0, gap), (0, 0))),
    )
    joined = own + arrived
    attended, rows = joined[0], joined[1]

    early = [k for k in range(n) if k < 4]
    late = [k for k in range(n) if k >= 4]

    def index_of(keys):
        return me ^ jnp.array(keys, jnp.int32)

    got = spread(attended)
    plain = (((1,), (0,)), ((), ()))
    turned = (((1,), (1,)), ((), ()))

    def out_block(w, s):
        return w.at[pl.ds(pl.multiple_of(s * share, share), share), :]

    out_args = (out_weight, out_block, (share, share), plain, share)
    acc = project([got[k] for k in early], index_of(early), *out_args, name="out_early")
    residual = project(
        [got[k] for k in late], index_of(late), *out_args, acc=acc, base=rows, name="out_late"
    )
    got = spread(residual)
    everyone = list(range(n))
    normed = norm([got[k] for k in everyone], index_of(everyone), ffn_gain)

    units = w_gate.shape[0]
    size = units // CHUNKS
    acc = None
    for c in range(CHUNKS):
        got = spread(hidden(normed, w_gate, w_up, c * size, size, size // 2))

        def down_block(w, s, c=c):
            return w.at[:, pl.ds(pl.multiple_of(s * units + c * size, 128), size)]

        for keys in (early, late):
            final = c == CHUNKS - 1 and keys is late
            acc = project(
                [got[k] for k in keys],
                index_of(keys),
                w_down,
                down_block,
                (share, size),
                turned,
                share,
                acc=acc,
                base=residual if final else None,
                name="down",
            )
    return acc


def per_device(*args):
    queries, counts = args[0], args[3]
    share = queries.shape[2]
    n = lax.axis_size("narrow")
    simple = (
        n == 8
        and lax.axis_size("wide") == 2
        and share % HEAD == 0
        and queries.shape[0] * 2 == counts.shape[0]
    )
    return local_device(*args) if simple else general_device(*args)


def solution(mesh):
    return jax.shard_map(
        per_device,
        mesh=mesh,
        in_specs=(
            P(("rep", "wide"), None, "narrow"),
            P(("rep", "wide"), None, "narrow"),
            P(("rep", "wide"), None),
            P("rep"),
            P(("rep", "wide"), "narrow", None),
            P(("rep", "wide"), "narrow", None),
            P(None, "narrow"),
            P(),
            P("narrow", None),
            P("narrow", None),
            P("narrow", None),
        ),
        out_specs=P(("rep", "wide"), "narrow"),
        check_vma=False,
    )
```

```python
import functools

import jax
import jax.numpy as jnp
from jax import lax
from jax.experimental import pallas as pl
from jax.experimental.pallas import tpu as pltpu
from jax.sharding import PartitionSpec as P


D = 4096
HEAD = 128
BAL = 150
CHUNKS = 3
WEIGH = 40

epsilon = 1e-05

BF = jnp.bfloat16
F32 = jnp.float32


def from_partner(x, axis, distance):
    return lax.ppermute(x, axis, [(i, i ^ 1 << distance) for i in range(lax.axis_size(axis))])


def rotate_queries(queries_f32, positions):
    half_size = HEAD // 2
    frequency = 500000.0 ** (-2.0 * jnp.arange(half_size, dtype=jnp.float32) / HEAD)
    angles = positions.astype(jnp.float32)[..., None] * frequency
    cosine_table = jnp.cos(angles)[..., None, :]
    sine_table = jnp.sin(angles)[..., None, :]
    lower_half = queries_f32[..., :half_size]
    upper_half = queries_f32[..., half_size:]
    return jnp.concatenate(
        [
            lower_half * cosine_table - upper_half * sine_table,
            upper_half * cosine_table + lower_half * sine_table,
        ],
        axis=-1,
    )


def balanced_slots(counts, canvases, slot_cap, groups, share):
    canvas_total = counts.shape[0]
    canvas_end = jnp.cumsum(counts, dtype=jnp.int32)
    canvas_start = canvas_end - counts
    global_slot = jnp.arange(groups * share, dtype=jnp.int32)
    canvas_of = jnp.sum(
        (canvas_end[None, :] <= global_slot[:, None]).astype(jnp.int32), axis=1, dtype=jnp.int32
    )
    canvas_of = jnp.minimum(canvas_of, canvas_total - 1)
    matches = canvas_of[:, None] == jnp.arange(canvas_total, dtype=jnp.int32)[None, :]
    picked_start = jnp.sum(jnp.where(matches, canvas_start[None, :], 0), axis=1, dtype=jnp.int32)
    within = global_slot - picked_start
    source = canvas_of // canvases
    local_slot = canvas_of % canvases * slot_cap + within
    return (source.reshape(groups, share), local_slot.reshape(groups, share))


def route_rows(rows_local, counts, canvases, slot_cap, groups, share):
    source, local_slot = balanced_slots(counts, canvases, slot_cap, groups, share)
    from_here = source == lax.axis_index("wide")
    picked = jnp.take(rows_local, jnp.where(from_here, local_slot, 0).reshape(-1), axis=0)
    picked = picked.reshape(groups, share, rows_local.shape[1])
    return jnp.where(from_here[:, :, None], picked, jnp.zeros_like(picked))


def feed_forward(residual, ffn_gain, w_gate, w_up, w_down):
    gathered = lax.all_gather(residual, "narrow", axis=1, tiled=True).astype(jnp.float32)
    normed = (
        gathered
        * lax.rsqrt(jnp.mean(gathered * gathered, axis=1, keepdims=True) + epsilon)
        * ffn_gain.astype(jnp.float32)
    ).astype(jnp.bfloat16)
    contract = (((1,), (1,)), ((), ()))
    gate_sum = lax.dot_general(normed, w_gate, contract, preferred_element_type=jnp.float32)
    up_sum = lax.dot_general(normed, w_up, contract, preferred_element_type=jnp.float32)
    activated = (jax.nn.silu(gate_sum) * up_sum).astype(jnp.bfloat16)
    output = lax.dot_general(
        lax.all_gather(activated, "narrow", axis=1, tiled=True),
        w_down,
        contract,
        preferred_element_type=jnp.float32,
    )
    return (residual.astype(jnp.float32) + output).astype(jnp.bfloat16)


def general_device(
    queries,
    layer_rows,
    positions,
    counts,
    key_cache,
    value_cache,
    out_weight,
    ffn_gain,
    w_gate,
    w_up,
    w_down,
):
    canvases, slot_cap, feature_share = queries.shape
    head_count = D // HEAD
    narrow_count = lax.axis_size("narrow")
    groups = lax.axis_size("wide")
    row_count = canvases * slot_cap
    group_size = max(1, narrow_count // head_count)
    local_heads = max(1, head_count // narrow_count)
    bit_steps = group_size.bit_length() - 1
    device_index = lax.axis_index("narrow")
    joined = queries
    for level in range(bit_steps):
        partner = from_partner(joined, "narrow", level)
        upper_bit = device_index // 2**level % 2 == 1
        joined = jnp.where(
            upper_bit,
            jnp.concatenate([partner, joined], axis=2),
            jnp.concatenate([joined, partner], axis=2),
        )
    rotated = rotate_queries(
        joined.astype(jnp.float32).reshape(canvases, slot_cap, local_heads, HEAD), positions
    ).astype(jnp.bfloat16)
    block_rows = key_cache.shape[1] // local_heads
    key_blocks = key_cache.reshape(canvases, local_heads, block_rows, HEAD)
    value_blocks = value_cache.reshape(canvases, local_heads, block_rows, HEAD)
    scores = jnp.einsum(
        "crhd,chpd->chrp", rotated, key_blocks, preferred_element_type=jnp.float32
    ) * HEAD ** (-0.5)
    row_peak = jnp.max(scores, axis=3)
    for level in range(bit_steps):
        other_peak = from_partner(row_peak, "narrow", level)
        row_peak = jnp.maximum(row_peak, other_peak)
    exponent = jnp.exp(scores - row_peak[..., None])
    totals = jnp.sum(exponent, axis=3)
    mixture = jnp.einsum(
        "chrp,chpd->crhd",
        exponent.astype(jnp.bfloat16),
        value_blocks,
        preferred_element_type=jnp.float32,
    ).reshape(row_count, local_heads * HEAD)
    for level in reversed(range(bit_steps)):
        half_width = mixture.shape[1] // 2
        lower_part = mixture[:, :half_width]
        upper_part = mixture[:, half_width:]
        upper_bit = device_index // 2**level % 2 == 1
        outgoing = jnp.where(upper_bit, lower_part, upper_part)
        kept = jnp.where(upper_bit, upper_part, lower_part)
        arrived, arrived_totals = from_partner((outgoing, totals), "narrow", level)
        mixture = kept + arrived
        totals = totals + arrived_totals
    divisor = jnp.repeat(
        jnp.transpose(totals, (0, 2, 1)).reshape(row_count, local_heads),
        mixture.shape[1] // local_heads,
        axis=1,
    )
    attended = (mixture / divisor).astype(jnp.bfloat16)
    projected = jnp.dot(
        lax.all_gather(attended, "narrow", axis=1, tiled=True),
        out_weight,
        preferred_element_type=jnp.float32,
    )
    residual = (
        layer_rows.reshape(row_count, feature_share).astype(jnp.float32) + projected
    ).astype(jnp.bfloat16)
    outgoing_rows = route_rows(residual, counts, canvases, slot_cap, groups, BAL)
    incoming = lax.all_to_all(outgoing_rows, "wide", split_axis=0, concat_axis=0, tiled=True)
    balanced = jnp.sum(incoming.astype(jnp.float32), axis=0).astype(jnp.bfloat16)
    return feed_forward(balanced, ffn_gain, w_gate, w_up, w_down)


def attend_kernel(
    slots, spill, counts, place, q_ref, cos_ref, sin_ref, k_ref, v_ref, rows_ref, own_ref, out_ref
):
    canvas = pl.program_id(1)
    canvases = pl.num_programs(1)
    wide = place[0]
    q = q_ref[0].astype(F32)
    half = HEAD // 2
    rotated = (q * cos_ref[0] + pltpu.roll(q, half, 1) * sin_ref[0]).astype(BF)
    scores = lax.dot_general(
        rotated, k_ref[0], (((1,), (1,)), ((), ())), preferred_element_type=F32
    ) * HEAD ** (-0.5)
    peak = jnp.max(scores, axis=1, keepdims=True)
    exponent = jnp.exp(scores - peak)
    total = jnp.sum(exponent, axis=1, keepdims=True)
    mixture = jnp.dot(exponent.astype(BF), v_ref[0], preferred_element_type=F32)
    attended = (mixture / total).astype(BF)

    mine = wide * canvases + canvas
    start = jnp.int32(0)
    for c in range(counts.shape[0]):
        start += jnp.where(c < mine, counts[c], 0)
    live = counts[mine]
    slot_cap = q.shape[0]

    def pick(size, shift):
        at = lax.broadcasted_iota(jnp.int32, (size, slot_cap), 0)
        slot = lax.broadcasted_iota(jnp.int32, (size, slot_cap), 1)
        return jnp.where((at == slot + shift) & (slot < live), 1.0, 0.0).astype(BF)

    pick_own = pick(slots, start - wide * slots)
    pick_out = pick(spill, start - (1 - wide) * slots - wide * (slots - spill))
    for i, value in enumerate((attended, rows_ref[0])):
        own = jnp.dot(pick_own, value, preferred_element_type=F32).astype(BF)
        out = jnp.dot(pick_out, value, preferred_element_type=F32).astype(BF)

        @pl.when(canvas == 0)
        def _():
            own_ref[i] = own
            out_ref[i] = out

        @pl.when(canvas > 0)
        def _():
            own_ref[i] += own
            out_ref[i] += out


def attend(queries, layer_rows, positions, counts, key_cache, value_cache, spill):
    canvases, slot_cap, features = queries.shape
    heads = features // HEAD
    length = key_cache.shape[1] // heads
    half = HEAD // 2
    frequency = 500000.0 ** (-2.0 * jnp.arange(half, dtype=F32) / HEAD)
    angles = positions.astype(F32)[..., None] * frequency
    cosine = jnp.cos(angles)
    sine = jnp.sin(angles)
    cosine = jnp.concatenate([cosine, cosine], axis=-1)
    sine = jnp.concatenate([-sine, sine], axis=-1)
    place = lax.axis_index("wide").astype(jnp.int32).reshape(1)
    table = pl.BlockSpec((1, slot_cap, HEAD), lambda h, c, *_: (c, 0, 0))
    rows = pl.BlockSpec((1, slot_cap, HEAD), lambda h, c, *_: (c, 0, h))
    cache = pl.BlockSpec((1, length, HEAD), lambda h, c, *_: (c, h, 0))
    return pl.pallas_call(
        functools.partial(attend_kernel, BAL, spill),
        grid_spec=pltpu.PrefetchScalarGridSpec(
            num_scalar_prefetch=2,
            grid=(heads, canvases),
            in_specs=[rows, table, table, cache, cache, rows],
            out_specs=[
                pl.BlockSpec((2, BAL, HEAD), lambda h, c, *_: (0, 0, h)),
                pl.BlockSpec((2, spill, HEAD), lambda h, c, *_: (0, 0, h)),
            ],
        ),
        out_shape=[
            jax.ShapeDtypeStruct((2, BAL, features), BF),
            jax.ShapeDtypeStruct((2, spill, features), BF),
        ],
        compiler_params=pltpu.CompilerParams(vmem_limit_bytes=24 << 20),
        cost_estimate=pl.CostEstimate(
            flops=4 * canvases * slot_cap * features * length,
            bytes_accessed=4 * canvases * heads * length * HEAD,
            transcendentals=canvases * slot_cap * heads * length,
        ),
        name="attend",
    )(counts, place, stay(queries), cosine, sine, stay(key_cache), stay(value_cache), stay(layer_rows))


def stay(x):
    return pltpu.with_memory_space_constraint(x, pltpu.HBM)


def project_kernel(n, block_of, contract, first, last, index, *refs):
    refs = list(refs)
    pieces = [refs.pop(0) for _ in range(n)]
    w_ref = refs.pop(0)
    acc_ref = None if first else refs.pop(0)
    base_ref = refs.pop(0) if last else None
    o_ref, held, sem = refs
    copies = []
    for i in range(n):
        copies.append(pltpu.make_async_copy(block_of(w_ref, index[i]), held.at[i], sem.at[i]))
        copies[-1].start()
    acc = None if first else acc_ref[...]
    for i in range(n):
        copies[i].wait()
        part = lax.dot_general(pieces[i][...], held[i], contract, preferred_element_type=F32)
        acc = part if acc is None else acc + part
    if last:
        acc = (base_ref[...].astype(F32) + acc).astype(BF)
    o_ref[...] = acc


def project(pieces, index, weight, block_of, block_shape, contract, columns, acc=None, base=None, weigh=1):
    n = len(pieces)
    rows = pieces[0].shape[0]
    vm = pl.BlockSpec(memory_space=pltpu.VMEM)
    operands = list(pieces) + [weight]
    specs = [vm] * n + [pl.BlockSpec(memory_space=pl.ANY)]
    for extra in (acc, base):
        if extra is not None:
            operands.append(extra)
            specs.append(vm)
    depth = pieces[0].shape[1]
    return pl.pallas_call(
        functools.partial(project_kernel, n, block_of, contract, acc is None, base is not None),
        in_specs=[pl.BlockSpec(memory_space=pltpu.SMEM)] + specs,
        out_specs=vm,
        out_shape=jax.ShapeDtypeStruct((rows, columns), F32 if base is None else BF),
        scratch_shapes=[
            pltpu.VMEM((n,) + block_shape, BF),
            pltpu.SemaphoreType.DMA((n,)),
        ],
        compiler_params=pltpu.CompilerParams(vmem_limit_bytes=24 << 20),
        cost_estimate=pl.CostEstimate(
            flops=2 * n * rows * depth * columns * weigh,
            bytes_accessed=2 * n * depth * columns,
            transcendentals=0,
        ),
    )(index, *operands)


def norm_kernel(n, index, *refs):
    pieces = refs[:n]
    gain_ref, o_ref = refs[n:]
    width = pieces[0].shape[1]
    total = 0.0
    for piece in pieces:
        value = piece[...].astype(F32)
        total = total + jnp.sum(value * value, axis=1, keepdims=True)
    scale = lax.rsqrt(total / (n * width) + epsilon)
    for i, piece in enumerate(pieces):
        at = pl.ds(pl.multiple_of(index[i] * width, width), width)
        value = piece[...].astype(F32) * scale * gain_ref[:, at].astype(F32)
        o_ref[:, at] = value.astype(BF)


def norm(pieces, index, gain):
    n = len(pieces)
    rows, width = pieces[0].shape
    vm = pl.BlockSpec(memory_space=pltpu.VMEM)
    return pl.pallas_call(
        functools.partial(norm_kernel, n),
        in_specs=[pl.BlockSpec(memory_space=pltpu.SMEM)] + [vm] * (n + 1),
        out_specs=vm,
        out_shape=jax.ShapeDtypeStruct((rows, n * width), BF),
        compiler_params=pltpu.CompilerParams(vmem_limit_bytes=24 << 20),
        cost_estimate=pl.CostEstimate(
            flops=6 * n * rows * width, bytes_accessed=4 * n * rows * width, transcendentals=rows
        ),
        name="norm",
    )(index, *pieces, gain.reshape(1, -1))


def hidden_kernel(x_ref, g_ref, u_ref, o_ref):
    contract = (((1,), (1,)), ((), ()))
    x = x_ref[...]
    gate = lax.dot_general(x, g_ref[...], contract, preferred_element_type=F32)
    up = lax.dot_general(x, u_ref[...], contract, preferred_element_type=F32)
    o_ref[...] = (gate / (1.0 + jnp.exp(-gate)) * up).astype(BF)


def hidden(normed, w_gate, w_up, begin, size, block):
    rows, depth = normed.shape
    weight = pl.BlockSpec((block, depth), lambda j: (begin // block + j, 0))
    return pl.pallas_call(
        hidden_kernel,
        grid=(size // block,),
        in_specs=[pl.BlockSpec((rows, depth), lambda j: (0, 0)), weight, weight],
        out_specs=pl.BlockSpec((rows, block), lambda j: (0, j)),
        out_shape=jax.ShapeDtypeStruct((rows, size), BF),
        compiler_params=pltpu.CompilerParams(vmem_limit_bytes=24 << 20),
        cost_estimate=pl.CostEstimate(
            flops=4 * rows * depth * size, bytes_accessed=4 * depth * size, transcendentals=rows * size
        ),
        name="hidden",
    )(normed, w_gate, w_up)


def permuted(x, k):
    return lax.ppermute(x, "narrow", [(i, i ^ k) for i in range(lax.axis_size("narrow"))])


def spread(x):
    n = lax.axis_size("narrow")
    pieces = {0: x}
    for k in range(2, n, 2):
        pieces[k] = permuted(x, k)
    for k in range(0, n, 2):
        pieces[k ^ 1] = permuted(pieces[k], 1)
    return pieces


def local_device(
    queries,
    layer_rows,
    positions,
    counts,
    key_cache,
    value_cache,
    out_weight,
    ffn_gain,
    w_gate,
    w_up,
    w_down,
):
    canvases, slot_cap, share = queries.shape
    n = lax.axis_size("narrow")
    me = lax.axis_index("narrow").astype(jnp.int32)
    wide = lax.axis_index("wide")
    spill = canvases * slot_cap - BAL
    own, out = attend(queries, layer_rows, positions, counts, key_cache, value_cache, spill)
    arrived = lax.ppermute(out, "wide", [(0, 1), (1, 0)])
    gap = BAL - spill
    arrived = jnp.where(
        wide == 0,
        jnp.pad(arrived, ((0, 0), (gap, 0), (0, 0))),
        jnp.pad(arrived, ((0, 0), (0, gap), (0, 0))),
    )
    joined = own + arrived
    attended, rows = joined[0], joined[1]

    early = [k for k in range(n) if k < 4]
    late = [k for k in range(n) if k >= 4]

    def index_of(keys):
        return me ^ jnp.array(keys, jnp.int32)

    got = spread(attended)
    plain = (((1,), (0,)), ((), ()))
    turned = (((1,), (1,)), ((), ()))

    def out_block(w, s):
        return w.at[pl.ds(pl.multiple_of(s * share, share), share), :]

    out_args = (out_weight, out_block, (share, share), plain, share)
    acc = project([got[k] for k in early], index_of(early), *out_args)
    residual = project(
        [got[k] for k in late], index_of(late), *out_args, acc=acc, base=rows, weigh=WEIGH
    )
    got = spread(residual)
    everyone = list(range(n))
    normed = norm([got[k] for k in everyone], index_of(everyone), ffn_gain)

    units = w_gate.shape[0]
    size = units // CHUNKS
    acc = None
    for c in range(CHUNKS):
        activated = hidden(normed, w_gate, w_up, c * size, size, size // 2)
        got = spread(activated)

        def down_block(w, s, c=c):
            return w.at[:, pl.ds(pl.multiple_of(s * units + c * size, 128), size)]

        for keys in (early, late):
            final = c == CHUNKS - 1 and keys is late
            acc = project(
                [got[k] for k in keys],
                index_of(keys),
                w_down,
                down_block,
                (share, size),
                turned,
                share,
                acc=acc,
                base=residual if final else None,
            )
    return acc


def per_device(*args):
    queries, counts = args[0], args[3]
    share = queries.shape[2]
    n = lax.axis_size("narrow")
    simple = (
        n == 8
        and lax.axis_size("wide") == 2
        and share % HEAD == 0
        and queries.shape[0] * 2 == counts.shape[0]
    )
    if not simple:
        return general_device(*args)
    return local_device(*args)


def solution(mesh):
    return jax.shard_map(
        per_device,
        mesh=mesh,
        in_specs=(
            P(("rep", "wide"), None, "narrow"),
            P(("rep", "wide"), None, "narrow"),
            P(("rep", "wide"), None),
            P("rep"),
            P(("rep", "wide"), "narrow", None),
            P(("rep", "wide"), "narrow", None),
            P(None, "narrow"),
            P(),
            P("narrow", None),
            P("narrow", None),
            P("narrow", None),
        ),
        out_specs=P(("rep", "wide"), "narrow"),
        check_vma=False,
    )
```

```python
import functools
import math

import jax
import jax.numpy as jnp
from jax import lax
from jax.experimental import pallas as pl
from jax.experimental.pallas import tpu as pltpu
from jax.sharding import PartitionSpec as P


D = 4096
HEAD = 128
BAL = 150
AHEAD = 3
CUTS = (4, 6, 2)
RELAYED = "pq"

epsilon = 1e-05

BF = jnp.bfloat16
F32 = jnp.float32


def from_partner(x, axis, distance):
    return lax.ppermute(x, axis, [(i, i ^ 1 << distance) for i in range(lax.axis_size(axis))])


def rotate_queries(queries_f32, positions):
    half_size = HEAD // 2
    frequency = 500000.0 ** (-2.0 * jnp.arange(half_size, dtype=jnp.float32) / HEAD)
    angles = positions.astype(jnp.float32)[..., None] * frequency
    cosine_table = jnp.cos(angles)[..., None, :]
    sine_table = jnp.sin(angles)[..., None, :]
    lower_half = queries_f32[..., :half_size]
    upper_half = queries_f32[..., half_size:]
    return jnp.concatenate(
        [
            lower_half * cosine_table - upper_half * sine_table,
            upper_half * cosine_table + lower_half * sine_table,
        ],
        axis=-1,
    )


def balanced_slots(counts, canvases, slot_cap, groups, share):
    canvas_total = counts.shape[0]
    canvas_end = jnp.cumsum(counts, dtype=jnp.int32)
    canvas_start = canvas_end - counts
    global_slot = jnp.arange(groups * share, dtype=jnp.int32)
    canvas_of = jnp.sum(
        (canvas_end[None, :] <= global_slot[:, None]).astype(jnp.int32), axis=1, dtype=jnp.int32
    )
    canvas_of = jnp.minimum(canvas_of, canvas_total - 1)
    matches = canvas_of[:, None] == jnp.arange(canvas_total, dtype=jnp.int32)[None, :]
    picked_start = jnp.sum(jnp.where(matches, canvas_start[None, :], 0), axis=1, dtype=jnp.int32)
    within = global_slot - picked_start
    source = canvas_of // canvases
    local_slot = canvas_of % canvases * slot_cap + within
    return (source.reshape(groups, share), local_slot.reshape(groups, share))


def route_rows(rows_local, counts, canvases, slot_cap, groups, share):
    source, local_slot = balanced_slots(counts, canvases, slot_cap, groups, share)
    from_here = source == lax.axis_index("wide")
    picked = jnp.take(rows_local, jnp.where(from_here, local_slot, 0).reshape(-1), axis=0)
    picked = picked.reshape(groups, share, rows_local.shape[1])
    return jnp.where(from_here[:, :, None], picked, jnp.zeros_like(picked))


def feed_forward(residual, ffn_gain, w_gate, w_up, w_down):
    gathered = lax.all_gather(residual, "narrow", axis=1, tiled=True).astype(jnp.float32)
    normed = (
        gathered
        * lax.rsqrt(jnp.mean(gathered * gathered, axis=1, keepdims=True) + epsilon)
        * ffn_gain.astype(jnp.float32)
    ).astype(jnp.bfloat16)
    contract = (((1,), (1,)), ((), ()))
    gate_sum = lax.dot_general(normed, w_gate, contract, preferred_element_type=jnp.float32)
    up_sum = lax.dot_general(normed, w_up, contract, preferred_element_type=jnp.float32)
    activated = (jax.nn.silu(gate_sum) * up_sum).astype(jnp.bfloat16)
    output = lax.dot_general(
        lax.all_gather(activated, "narrow", axis=1, tiled=True),
        w_down,
        contract,
        preferred_element_type=jnp.float32,
    )
    return (residual.astype(jnp.float32) + output).astype(jnp.bfloat16)


def general_device(
    queries,
    layer_rows,
    positions,
    counts,
    key_cache,
    value_cache,
    out_weight,
    ffn_gain,
    w_gate,
    w_up,
    w_down,
):
    canvases, slot_cap, feature_share = queries.shape
    head_count = D // HEAD
    narrow_count = lax.axis_size("narrow")
    groups = lax.axis_size("wide")
    row_count = canvases * slot_cap
    group_size = max(1, narrow_count // head_count)
    local_heads = max(1, head_count // narrow_count)
    bit_steps = group_size.bit_length() - 1
    device_index = lax.axis_index("narrow")
    joined = queries
    for level in range(bit_steps):
        partner = from_partner(joined, "narrow", level)
        upper_bit = device_index // 2**level % 2 == 1
        joined = jnp.where(
            upper_bit,
            jnp.concatenate([partner, joined], axis=2),
            jnp.concatenate([joined, partner], axis=2),
        )
    rotated = rotate_queries(
        joined.astype(jnp.float32).reshape(canvases, slot_cap, local_heads, HEAD), positions
    ).astype(jnp.bfloat16)
    block_rows = key_cache.shape[1] // local_heads
    key_blocks = key_cache.reshape(canvases, local_heads, block_rows, HEAD)
    value_blocks = value_cache.reshape(canvases, local_heads, block_rows, HEAD)
    scores = jnp.einsum(
        "crhd,chpd->chrp", rotated, key_blocks, preferred_element_type=jnp.float32
    ) * HEAD ** (-0.5)
    row_peak = jnp.max(scores, axis=3)
    for level in range(bit_steps):
        other_peak = from_partner(row_peak, "narrow", level)
        row_peak = jnp.maximum(row_peak, other_peak)
    exponent = jnp.exp(scores - row_peak[..., None])
    totals = jnp.sum(exponent, axis=3)
    mixture = jnp.einsum(
        "chrp,chpd->crhd",
        exponent.astype(jnp.bfloat16),
        value_blocks,
        preferred_element_type=jnp.float32,
    ).reshape(row_count, local_heads * HEAD)
    for level in reversed(range(bit_steps)):
        half_width = mixture.shape[1] // 2
        lower_part = mixture[:, :half_width]
        upper_part = mixture[:, half_width:]
        upper_bit = device_index // 2**level % 2 == 1
        outgoing = jnp.where(upper_bit, lower_part, upper_part)
        kept = jnp.where(upper_bit, upper_part, lower_part)
        arrived, arrived_totals = from_partner((outgoing, totals), "narrow", level)
        mixture = kept + arrived
        totals = totals + arrived_totals
    divisor = jnp.repeat(
        jnp.transpose(totals, (0, 2, 1)).reshape(row_count, local_heads),
        mixture.shape[1] // local_heads,
        axis=1,
    )
    attended = (mixture / divisor).astype(jnp.bfloat16)
    projected = jnp.dot(
        lax.all_gather(attended, "narrow", axis=1, tiled=True),
        out_weight,
        preferred_element_type=jnp.float32,
    )
    residual = (
        layer_rows.reshape(row_count, feature_share).astype(jnp.float32) + projected
    ).astype(jnp.bfloat16)
    outgoing_rows = route_rows(residual, counts, canvases, slot_cap, groups, BAL)
    incoming = lax.all_to_all(outgoing_rows, "wide", split_axis=0, concat_axis=0, tiled=True)
    balanced = jnp.sum(incoming.astype(jnp.float32), axis=0).astype(jnp.bfloat16)
    return feed_forward(balanced, ffn_gain, w_gate, w_up, w_down)


def attend_kernel(
    slots,
    spill,
    place,
    frequency_ref,
    positions_hbm,
    counts_hbm,
    queries_hbm,
    rows_hbm,
    keys_hbm,
    values_hbm,
    own_ref,
    out_ref,
    positions,
    counts,
    queries,
    rows,
    keys,
    values,
    attended,
    cosine,
    sine,
    scores,
    sems,
    key_sems,
    value_sems,
):
    canvases, slot_cap, features = queries.shape
    heads = features // HEAD
    length = keys.shape[1] // heads
    half = HEAD // 2
    wide = place[0]

    def copy(source, target, sem):
        started = pltpu.make_async_copy(source, target, sem)
        started.start()
        return started

    positions_copy = copy(positions_hbm, positions, sems.at[0])
    queries_copy = copy(queries_hbm, queries, sems.at[1])
    units = [(h, c) for h in range(heads) for c in range(canvases)]
    key_copies, value_copies = {}, {}

    def fetch(i):
        if i < len(units):
            h, c = units[i]
            at = pl.ds(h * length, length)
            key_copies[i] = copy(keys_hbm.at[c, at], keys.at[c, at], key_sems.at[i])
            value_copies[i] = copy(values_hbm.at[c, at], values.at[c, at], value_sems.at[i])

    for i in range(AHEAD):
        fetch(i)
    rows_copy = copy(rows_hbm, rows, sems.at[2])
    counts_copy = copy(counts_hbm, counts, sems.at[3])

    positions_copy.wait()
    square = (slot_cap, slot_cap)
    diagonal = lax.broadcasted_iota(jnp.int32, square, 0) == lax.broadcasted_iota(
        jnp.int32, square, 1
    )
    sign = jnp.where(lax.broadcasted_iota(jnp.int32, (1, HEAD), 1) < half, -1.0, 1.0)
    for c in range(canvases):
        at = positions[c : c + 1, :].astype(F32)
        angle = jnp.sum(jnp.where(diagonal, at, 0.0), axis=1, keepdims=True) * frequency_ref[...]
        cosine[c] = jnp.cos(angle)
        sine[c] = jnp.sin(angle) * sign
    queries_copy.wait()

    def score(i):
        h, c = units[i]
        q = queries[c, :, h * HEAD : (h + 1) * HEAD].astype(F32)
        rotated = (q * cosine[c] + pltpu.roll(q, half, 1) * sine[c]).astype(BF)
        key_copies[i].wait()
        fetch(i + AHEAD)
        scores[i % 2] = lax.dot_general(
            rotated,
            keys[c, h * length : (h + 1) * length, :],
            (((1,), (1,)), ((), ())),
            preferred_element_type=F32,
        )

    def mix(i):
        h, c = units[i]
        s = scores[i % 2]
        peak = jnp.max(s, axis=1, keepdims=True)
        exponent = jnp.exp2((s - peak) * (HEAD ** (-0.5) * math.log2(math.e)))
        total = jnp.sum(exponent, axis=1, keepdims=True)
        value_copies[i].wait()
        mixture = jnp.dot(
            exponent.astype(BF),
            values[c, h * length : (h + 1) * length, :],
            preferred_element_type=F32,
        )
        attended[c, :, h * HEAD : (h + 1) * HEAD] = (mixture / total).astype(BF)

    score(0)
    for i in range(1, len(units)):
        score(i)
        mix(i - 1)
    mix(len(units) - 1)

    rows_copy.wait()
    counts_copy.wait()
    own, out = [0.0, 0.0], [0.0, 0.0]
    for c in range(canvases):
        mine = wide * canvases + c
        start = jnp.int32(0)
        for i in range(counts.shape[0]):
            start += jnp.where(i < mine, counts[i], 0)
        live = counts[mine]

        def pick(size, shift):
            at = lax.broadcasted_iota(jnp.int32, (size, slot_cap), 0)
            slot = lax.broadcasted_iota(jnp.int32, (size, slot_cap), 1)
            return jnp.where((at == slot + shift) & (slot < live), 1.0, 0.0).astype(BF)

        pick_own = pick(slots, start - wide * slots)
        pick_out = pick(spill, start - (1 - wide) * slots - wide * (slots - spill))
        for i, held in enumerate((attended, rows)):
            own[i] += jnp.dot(pick_own, held[c], preferred_element_type=F32)
            out[i] += jnp.dot(pick_out, held[c], preferred_element_type=F32)
    for i in range(2):
        own_ref[i] = own[i].astype(BF)
        out_ref[i] = out[i].astype(BF)


def attend(queries, layer_rows, positions, counts, key_cache, value_cache, spill):
    canvases, slot_cap, features = queries.shape
    heads = features // HEAD
    length = key_cache.shape[1] // heads
    half = HEAD // 2
    frequency = 500000.0 ** (-2.0 * jnp.arange(half, dtype=F32) / HEAD)
    frequency = jnp.concatenate([frequency, frequency]).reshape(1, HEAD)
    place = lax.axis_index("wide").astype(jnp.int32).reshape(1)
    operands = (positions, counts, queries, layer_rows, key_cache, value_cache)
    inside = pl.BlockSpec(memory_space=pltpu.VMEM)
    units = heads * canvases
    return pl.pallas_call(
        functools.partial(attend_kernel, BAL, spill),
        in_specs=[pl.BlockSpec(memory_space=pltpu.SMEM), inside]
        + [pl.BlockSpec(memory_space=pl.ANY)] * len(operands),
        out_specs=[inside, inside],
        out_shape=[
            jax.ShapeDtypeStruct((2, BAL, features), BF),
            jax.ShapeDtypeStruct((2, spill, features), BF),
        ],
        scratch_shapes=[
            pltpu.VMEM(positions.shape, jnp.int32),
            pltpu.SMEM(counts.shape, jnp.int32),
            pltpu.VMEM(queries.shape, BF),
            pltpu.VMEM(layer_rows.shape, BF),
            pltpu.VMEM(key_cache.shape, BF),
            pltpu.VMEM(value_cache.shape, BF),
            pltpu.VMEM(queries.shape, BF),
            pltpu.VMEM((canvases, slot_cap, HEAD), F32),
            pltpu.VMEM((canvases, slot_cap, HEAD), F32),
            pltpu.VMEM((2, slot_cap, length), F32),
            pltpu.SemaphoreType.DMA((4,)),
            pltpu.SemaphoreType.DMA((units,)),
            pltpu.SemaphoreType.DMA((units,)),
        ],
        compiler_params=pltpu.CompilerParams(vmem_limit_bytes=20 << 20),
        cost_estimate=pl.CostEstimate(
            flops=4 * canvases * slot_cap * features * length,
            bytes_accessed=4 * key_cache.size,
            transcendentals=canvases * slot_cap * heads * length,
        ),
        name="attend",
    )(place, frequency, *[stay(x) for x in operands])


class Places:
    def __init__(self, keys, me):
        self.keys, self.me = keys, me

    def __getitem__(self, i):
        return self.me[0] ^ self.keys[i]


def stay(x):
    return pltpu.with_memory_space_constraint(x, pltpu.HBM)


def project_kernel(terms, block_of, contract, first, last, keys, me, *refs):
    refs, index = list(refs), Places(keys, me)
    arrays = [refs.pop(0) for _ in range(1 + max(max(which) for which, _ in terms))]
    w_ref = refs.pop(0)
    acc_ref = None if first else refs.pop(0)
    base_ref = refs.pop(0) if last else None
    (o_ref,) = refs
    acc = None if first else acc_ref[...]
    for i, (which, part) in enumerate(terms):
        values = [arrays[j][...] if part is None else arrays[j][part] for j in which]
        value = values[0]
        if len(values) > 1:
            value = (values[0].astype(F32) + values[1].astype(F32)).astype(BF)
        block = block_of(w_ref, index[i])[...]
        product = lax.dot_general(value, block, contract, preferred_element_type=F32)
        acc = product if acc is None else acc + product
    if last:
        acc = (base_ref[...].astype(F32) + acc).astype(BF)
    o_ref[...] = acc


def project(terms, index, weight, block_of, contract, columns, acc=None, base=None):
    operands, forms = [], []
    for arrays, part in terms:
        which = []
        for x in arrays:
            known = [j for j, y in enumerate(operands) if y is x]
            if not known:
                operands.append(x)
            which.append(known[0] if known else len(operands) - 1)
        forms.append((tuple(which), part))
    n = len(terms)
    rows, depth = operands[0].shape[-2:]
    operands.append(weight)
    operands.extend(extra for extra in (acc, base) if extra is not None)
    vm = pl.BlockSpec(memory_space=pltpu.VMEM)
    return pl.pallas_call(
        functools.partial(
            project_kernel, tuple(forms), block_of, contract, acc is None, base is not None, index[1]
        ),
        in_specs=[pl.BlockSpec(memory_space=pltpu.SMEM)] + [vm] * len(operands),
        out_specs=vm,
        out_shape=jax.ShapeDtypeStruct((rows, columns), F32 if base is None else BF),
        compiler_params=pltpu.CompilerParams(vmem_limit_bytes=16 << 20),
        cost_estimate=pl.CostEstimate(
            flops=2 * n * rows * depth * columns,
            bytes_accessed=2 * n * depth * columns,
            transcendentals=0,
        ),
    )(index[0], *operands)


SLOTS = 3


def square_sum(value):
    return jnp.sum(value * value, axis=1, keepdims=True)


def scaled(piece_ref, gain_ref, place):
    width = piece_ref.shape[1]
    value = piece_ref[...].astype(F32)
    at = pl.ds(pl.multiple_of(place * width, width), width)
    return value, (value * gain_ref[:, at].astype(F32)).astype(BF)


def blend_kernel(origins, first, keys, me, *refs):
    refs, index = list(refs), Places(keys, me)
    pieces = [refs.pop(0) for _ in origins]
    gain_ref = refs.pop(0)
    weights = [refs.pop(0), refs.pop(0)]
    kept = refs.pop(0)
    before = None if first else [refs.pop(0) for _ in range(3)]
    sums = [refs.pop(0), refs.pop(0)]
    square_ref, held, sems = refs
    width = pieces[0].shape[1]
    slots = held.shape[0]
    steps = [(i, w) for i in range(len(origins)) for w in range(2)]
    moved = [step for step in steps if origins[step[0]] < 0]
    copies = {}

    def begin(j):
        if j < len(moved):
            i, w = moved[j]
            at = pl.ds(pl.multiple_of(index[i] * width, width), width)
            copies[moved[j]] = pltpu.make_async_copy(
                weights[w].at[:, at], held.at[j % slots], sems.at[j]
            )
            copies[moved[j]].start()

    for j in range(slots):
        begin(j)
    square = 0.0 if first else before[2][...]
    for i, w in steps:
        if w == 0:
            value, x = scaled(pieces[i], gain_ref, index[i])
            square = square + square_sum(value)
        if (i, w) in moved:
            j = moved.index((i, w))
            copies[i, w].wait()
            weight = held[j % slots]
        else:
            weight = kept[w, origins[i]]
        product = lax.dot_general(
            x, weight, (((1,), (1,)), ((), ())), preferred_element_type=F32
        )
        if i > 0:
            product = product + sums[w][...]
        elif not first:
            product = product + before[w][...]
        sums[w][...] = product
        if (i, w) in moved:
            begin(j + slots)
    square_ref[...] = jnp.broadcast_to(square, square_ref.shape)


def blend(pieces, origins, index, gain, w_gate, w_up, kept, before=None):
    n = len(pieces)
    rows, width = pieces[0].shape
    units = w_gate.shape[0]
    vm = pl.BlockSpec(memory_space=pltpu.VMEM)
    hbm = pl.BlockSpec(memory_space=pl.ANY)
    moved = sum(2 for m in origins if m < 0)
    return pl.pallas_call(
        functools.partial(blend_kernel, origins, before is None, index[1]),
        in_specs=[pl.BlockSpec(memory_space=pltpu.SMEM)]
        + [vm] * (n + 1)
        + [hbm] * 2
        + [vm] * (1 if before is None else 4),
        out_specs=[vm] * 3,
        out_shape=[jax.ShapeDtypeStruct((rows, units), F32)] * 2
        + [jax.ShapeDtypeStruct((rows, HEAD), F32)],
        scratch_shapes=[
            pltpu.VMEM((min(SLOTS, moved), units, width), BF),
            pltpu.SemaphoreType.DMA((moved,)),
        ],
        compiler_params=pltpu.CompilerParams(vmem_limit_bytes=24 << 20),
        cost_estimate=pl.CostEstimate(
            flops=4 * n * rows * width * units,
            bytes_accessed=4 * n * width * units,
            transcendentals=0,
        ),
    )(index[0], *pieces, gain, stay(w_gate), stay(w_up), kept, *(before or ()))


def keep_kernel(keys, me, *refs):
    n, index = len(keys), Places(keys, me)
    gate_hbm, up_hbm, kept, sems = refs
    width = kept.shape[3]
    copies = []
    for i in range(n):
        at = pl.ds(pl.multiple_of(index[i] * width, width), width)
        for w, source in enumerate((gate_hbm, up_hbm)):
            copies.append(
                pltpu.make_async_copy(source.at[:, at], kept.at[w, i], sems.at[w, i])
            )
            copies[-1].start()
    for started in copies:
        started.wait()


def keep(index, w_gate, w_up, width):
    n = len(index[1])
    hbm = pl.BlockSpec(memory_space=pl.ANY)
    shape = (2, n, w_gate.shape[0], width)
    return pl.pallas_call(
        functools.partial(keep_kernel, index[1]),
        in_specs=[pl.BlockSpec(memory_space=pltpu.SMEM), hbm, hbm],
        out_specs=pl.BlockSpec(memory_space=pltpu.VMEM),
        out_shape=pltpu.VMEM(shape, BF),
        scratch_shapes=[pltpu.SemaphoreType.DMA((2, n))],
        compiler_params=pltpu.CompilerParams(vmem_limit_bytes=16 << 20),
        cost_estimate=pl.CostEstimate(
            flops=0, bytes_accessed=4 * n * w_gate.shape[0] * width, transcendentals=0
        ),
    )(index[0], stay(w_gate), stay(w_up))


def hidden_kernel(n, begin, size, features, skip, keys, me, *refs):
    index = Places(keys, me)
    pieces = refs[:n]
    gain_ref, gate_ref, up_ref, square_ref, kept, o_ref = refs[n:]
    at = slice(begin, begin + size)
    square = square_ref[:, :1]
    gate, up = gate_ref[:, at], up_ref[:, at]
    contract = (((1,), (1,)), ((), ()))
    for i in range(n):
        value, x = scaled(pieces[i], gain_ref, index[i])
        square = square + square_sum(value)
        gate = gate + lax.dot_general(x, kept[0, skip + i, at, :], contract, preferred_element_type=F32)
        up = up + lax.dot_general(x, kept[1, skip + i, at, :], contract, preferred_element_type=F32)
    scale = lax.rsqrt(square / features + epsilon)
    gate = gate * scale
    o_ref[...] = (gate / (1.0 + jnp.exp(-gate)) * (up * scale)).astype(BF)


def hidden(pieces, index, gain, sums, kept, begin, size):
    rows, width = pieces[0].shape
    vm = pl.BlockSpec(memory_space=pltpu.VMEM)
    n = len(pieces)
    return pl.pallas_call(
        functools.partial(
            hidden_kernel, n, begin, size, gain.shape[1], kept.shape[1] - n, index[1]
        ),
        in_specs=[pl.BlockSpec(memory_space=pltpu.SMEM)] + [vm] * (n + 5),
        out_specs=vm,
        out_shape=jax.ShapeDtypeStruct((rows, size), BF),
        compiler_params=pltpu.CompilerParams(vmem_limit_bytes=16 << 20),
        cost_estimate=pl.CostEstimate(
            flops=4 * n * rows * width * size,
            bytes_accessed=4 * n * width * size,
            transcendentals=rows * size,
        ),
        name="hidden",
    )(index[0], *pieces, gain, *sums, kept)


def permuted(x, pairs):
    return lax.ppermute(x, "narrow", pairs)


def across(k):
    return [(i, i ^ k) for i in range(lax.axis_size("narrow"))]


MIDDLE = [(2, 4), (3, 5), (4, 2), (5, 3)]
ENDS = [(2, 0), (3, 1), (4, 6), (5, 7)]


def spread(x):
    pieces = {0: x}
    for k in (2, 4, 6):
        pieces[k] = permuted(x, across(k))
    for k in (0, 2, 4, 6):
        pieces[k ^ 1] = permuted(pieces[k], across(1))
    return pieces


def relay(x, tag):
    near = permuted(x, across(2))
    if tag not in RELAYED:
        far = permuted(x, across(4))
        return near, far, (permuted(x, across(6)),)
    middle = permuted(x, MIDDLE)
    far = permuted(x, across(4))
    ends = permuted(far, ENDS)
    return near, far, (middle, ends)


def merged(pair):
    if len(pair) == 1:
        return pair[0]
    return (pair[0].astype(F32) + pair[1].astype(F32)).astype(BF)


def local_device(
    queries,
    layer_rows,
    positions,
    counts,
    key_cache,
    value_cache,
    out_weight,
    ffn_gain,
    w_gate,
    w_up,
    w_down,
):
    canvases, slot_cap, share = queries.shape
    me = lax.axis_index("narrow").astype(jnp.int32).reshape(1)
    wide = lax.axis_index("wide")
    spill = canvases * slot_cap - BAL
    own, out = attend(queries, layer_rows, positions, counts, key_cache, value_cache, spill)
    arrived = lax.ppermute(out, "wide", [(0, 1), (1, 0)])
    gap = BAL - spill
    arrived = jnp.where(
        wide == 0,
        jnp.pad(arrived, ((0, 0), (gap, 0), (0, 0))),
        jnp.pad(arrived, ((0, 0), (0, gap), (0, 0))),
    )
    joined = own + arrived
    attended, rows = joined[0], joined[1]

    def index_of(*keys):
        return me, keys

    plain = (((1,), (0,)), ((), ()))
    turned = (((1,), (1,)), ((), ()))

    def out_block(w, s):
        return w.at[pl.ds(pl.multiple_of(s * share, share), share), :]

    near_weight = out_weight
    kept = keep(index_of(4, 6, 5, 7), w_gate, w_up, share)
    got = spread(attended)
    acc = None
    for keys, name in (((0, 1, 2, 3), "oute"), ((4, 5, 6, 7), "outl")):
        acc = project(
            [((got[k],), None) for k in keys],
            index_of(*keys),
            near_weight,
            out_block,
            plain,
            share,
            acc=acc,
            base=rows if name == "outl" else None,
        )
    residual = acc

    got = spread(residual)
    gain = ffn_gain.reshape(1, -1)
    weights = (w_gate, w_up, kept)
    sums = blend([got[k] for k in (0, 1, 2)], (-1, -1, -1), index_of(0, 1, 2), gain, *weights)
    sums = blend(
        [got[k] for k in (3, 4, 6)], (-1, 0, 1), index_of(3, 4, 6), gain, *weights, before=sums
    )

    units = w_gate.shape[0]
    cuts, begin = {}, 0
    for tag, share_of in zip("pqr", CUTS):
        size = share_of * units // sum(CUTS)
        cuts[tag] = (begin, size)
        begin += size
    active = {
        tag: hidden([got[5], got[7]], index_of(5, 7), gain, sums, kept, *cuts[tag])
        for tag in cuts
    }

    acc = None
    down_weight = w_down

    def down(tag, terms, keys, final=False):
        begin, size = cuts[tag]

        def down_block(w, s):
            return w.at[:, pl.ds(pl.multiple_of(s * units + begin, HEAD), size)]

        return project(
            terms,
            index_of(*keys),
            down_weight,
            down_block,
            turned,
            share,
            acc=acc,
            base=residual if final else None,
        )

    late = {}
    for tag in ("p", "q"):
        x = active[tag]
        near, far, pair = relay(x, tag)
        third = merged(pair)
        there = [permuted(y, across(1)) for y in (x, near, far, third)]
        here = [x, near, far, third]
        early = [((y,), None) for y in (here[0], here[1], there[0], there[1])]
        late[tag] = [((y,), None) for y in (here[2], here[3], there[2], there[3])]
        if tag == "q":
            acc = down("p", late["p"], (4, 6, 5, 7))
        acc = down(tag, early, (0, 2, 1, 3))
    both = jnp.stack([active["r"], permuted(active["r"], across(1))])
    near, far, pair = relay(both, "r")
    terms = [((x,), part) for x in (both, near, far) for part in (0, 1)]
    terms += [(pair, 0), (pair, 1)]
    acc = down("q", late["q"][:3], (4, 6, 5))
    acc = down("r", terms, (0, 1, 2, 3, 4, 5, 6, 7))
    return down("q", late["q"][3:], (7,), final=True)


def per_device(*args):
    queries, counts = args[0], args[3]
    share = queries.shape[2]
    n = lax.axis_size("narrow")
    simple = (
        n == 8
        and lax.axis_size("wide") == 2
        and share % HEAD == 0
        and queries.shape[0] * 2 == counts.shape[0]
    )
    if not simple:
        return general_device(*args)
    return local_device(*args)


def solution(mesh):
    program = jax.shard_map(
        per_device,
        mesh=mesh,
        in_specs=(
            P(("rep", "wide"), None, "narrow"),
            P(("rep", "wide"), None, "narrow"),
            P(("rep", "wide"), None),
            P("rep"),
            P(("rep", "wide"), "narrow", None),
            P(("rep", "wide"), "narrow", None),
            P(None, "narrow"),
            P(),
            P("narrow", None),
            P("narrow", None),
            P("narrow", None),
        ),
        out_specs=P(("rep", "wide"), "narrow"),
        check_vma=False,
    )
    if mesh.shape["narrow"] != 8:
        return program
    return program
```
